32 devices in a mesh: ja: 8 (over z, y), pt: 4 (over x, core).
Axes of the slice: x: 2, y: 2, z: 4, core: 2. Of those that a mesh axis runs over, the one named last changes fastest.
Arguments:
- amplitudes: bfloat16 [8, 4, 3072, 512], P('ja', 'pt'), may hold values from -6 to 6
- live_rows: int32 [8, 4], P('ja', 'pt'), may hold values from 384 to 3072, as said below
- hole_coupling: bfloat16 [8, 4, 3, 512, 512], P('ja', 'pt'), may hold values from -0.25 to 0.25
- part_hole: bfloat16 [8, 4, 3072, 512], P('ja', 'pt'), may hold values from -0.0048828125 to 0.0048828125
- recoupling: float32 [8, 3], replicated, may hold values from -1 to 1
Outputs:
- operator_bar: bfloat16 [8, 4, 3072, 512], P('ja', 'pt')
The draws below stay inside these ranges and needn't reach their ends.
Inputs may be any that keep to these rules, and one draw needn't show every extreme that they name: `live_rows`: rows in use of a channel; some channel has exactly 3072.
All inputs are finite; a program needn't handle non-finite values.
Results may differ from the reference program's by a relative error of at most 0.0085.
Values may be sent and summed in bfloat16 or wider, within the bound.
A program may use at most 128 MiB of HBM per device.

```python
import jax
import jax.numpy as jnp
import numpy as np
from jax import lax

H = 512
P_SIZE = 3072
NJ = 8


def draw_live_rows(key, part):
    first_key, second_key = jax.random.split(jax.random.fold_in(key, 17))
    values = jax.random.randint(first_key, (NJ * 4,), P_SIZE // 8, P_SIZE + 1, dtype=jnp.int32)
    chosen = jax.random.randint(second_key, (), 0, NJ * 4, dtype=jnp.int32)
    values = jnp.where(jnp.arange(NJ * 4, dtype=jnp.int32) == chosen, P_SIZE, values)
    return values.reshape(NJ, 4).astype(jnp.int32)


def level_of(own_key, extent, shards, smallest, largest):
    def one(dim, parts):
        heights = jax.random.uniform(jax.random.fold_in(jax.random.fold_in(own_key, 6), dim), (parts,), jnp.float32, smallest / len(shards), largest / len(shards))
        return jnp.repeat(jnp.exp(heights), extent[dim] // parts).reshape((-1,) + (1,) * (len(extent) - dim - 1))

    loudness = one(*shards[0])
    for cut in shards[1:]:
        loudness = loudness * one(*cut)
    return loudness


def noise(key, dims, scale, limit, pieces=(), kind=jnp.bfloat16):
    loudness = level_of(key, dims, pieces, -0.22, 0.18) if pieces else 1.0
    values = jax.random.normal(key, dims, jnp.float32) * scale * loudness
    return jnp.minimum(jnp.maximum(values, -limit), limit).astype(kind)


def setup_inputs(seed: int = 0) -> dict:
    seeds = jax.random.split(jax.random.key(seed), 6)
    amplitudes = noise(seeds[0], (NJ, 4, P_SIZE, H), 1.0, 6.0, ((0, 8), (1, 4)))
    live_rows = draw_live_rows(jax.random.fold_in(seeds[5], 71), 0)
    hole_coupling = noise(seeds[2], (NJ, 4, 3, H, H), H ** -0.5, 0.25, ((0, 8), (1, 4)))
    part_hole = noise(seeds[3], (NJ, 4, P_SIZE, H), (P_SIZE * H) ** -0.5, 0.0048828125, ((0, 8), (1, 4)))
    recoupling = jnp.clip(jax.random.uniform(seeds[4], (NJ, 3), jnp.float32, -1.0, 1.0), -1.0, 1.0)
    return dict(amplitudes=amplitudes, live_rows=live_rows, hole_coupling=hole_coupling, part_hole=part_hole, recoupling=recoupling)


def segment_weights(recoupling):
    chan_total = recoupling.shape[0]
    half_count = chan_total // 2
    position = jnp.arange(chan_total, dtype=jnp.int32) % half_count
    keep = jnp.stack([position > 0, position >= 0, position < half_count - 1], axis=1)
    return jnp.where(keep, recoupling, jnp.zeros((), recoupling.dtype))


def reference(amplitudes, live_rows, hole_coupling, part_hole, recoupling):
    chan_total = amplitudes.shape[0]
    row_count = amplitudes.shape[2]
    hole_count = amplitudes.shape[3]
    partner = np.array([2, 3, 0, 1])
    row_ids = jnp.arange(row_count, dtype=jnp.int32)
    weights_all = segment_weights(recoupling)

    def masked(index):
        live_mask = row_ids[None, :] < live_rows[index][:, None]
        return jnp.where(live_mask[:, :, None], amplitudes[index], jnp.zeros((), amplitudes.dtype))

    def intermediate(index):
        return jnp.einsum("qph,qpk->qhk", masked(index).astype(jnp.float32),
                          part_hole[index].astype(jnp.float32)).astype(jnp.bfloat16)

    inter_hh = lax.map(intermediate, jnp.arange(chan_total, dtype=jnp.int32))

    def target(index):
        term_sum = jnp.zeros((4, row_count, hole_count), jnp.float32)
        mixing = jnp.zeros((4, hole_count, hole_count), jnp.float32)
        for offset in range(3):
            source_j = index + offset - 1
            valid = (source_j >= 0) & (source_j < chan_total)
            clipped = jnp.clip(source_j, 0, chan_total - 1).astype(jnp.int32)
            factor = jnp.where(valid, weights_all[clipped, 2 - offset], jnp.zeros((), recoupling.dtype))
            source = masked(clipped)[partner].astype(jnp.float32)
            hole_block = hole_coupling[clipped][partner][:, 2 - offset].astype(jnp.float32)
            term_sum = term_sum + factor * jnp.einsum("qph,qhk->qpk", source, hole_block)
            mixing = mixing + factor * inter_hh[clipped][partner].astype(jnp.float32)
        mix_bf = mixing.astype(jnp.bfloat16)
        own = masked(index)
        term_sum = term_sum + jnp.einsum("qph,qhk->qpk", own.astype(jnp.float32), mix_bf.astype(jnp.float32))
        live_mask = row_ids[None, :] < live_rows[index][:, None]
        return jnp.where(live_mask[:, :, None], term_sum, jnp.zeros((), term_sum.dtype)).astype(jnp.bfloat16)

    return lax.map(target, jnp.arange(chan_total, dtype=jnp.int32))
```

```python
import functools

import jax
import jax.numpy as jnp
from jax import lax
from jax.experimental import pallas as pl
from jax.experimental.pallas import tpu as pltpu
from jax.sharding import PartitionSpec as P

MESH = pl.DeviceIdType.MESH
CHUNK = 128
BLOCK = 512
HEAD = 3
GAP = 2
LAG = 9


def kernel(
    half, chunk, block, raw,
    wts, live, amp_hbm, hole_hbm, part_hbm, out,
    amp, hole, part, acc, inter, mix_in, raw_in, fwd_in, cfar_in, cnear_out, cnear_in, mix,
    far_out, far_in, near_out, near_in, side_out, side_in, near_p, side_p,
    amp_sem, part_sem, hole_sem,
    far_s, far_r, near_s, near_r, side_s, side_r, inter_s, inter_r,
    raw_s, raw_r, fwd_s, fwd_r, cfar_s, cfar_r, cnear_s, cnear_r,
):
    rows, holes = amp.shape
    terms = rows // chunk
    blocks = rows // block
    mixes, _, width = inter.shape
    tail = mixes - raw
    wide = raw * width
    quarter, mid = chunk // 4, chunk // 2
    subs = [(i * quarter, quarter) for i in range(4)] + [(chunk + i * mid, mid) for i in range(2)]
    first_items = {0: range(0, 4), 1: range(4, 6)}

    chans = wts.shape[1]
    chan = lax.axis_index("ja")
    label = lax.axis_index("pt")
    pos = lax.rem(chan, half)
    base = chan - pos
    odd = lax.rem(chan, 2)
    sign = 2 * odd - 1
    near = chan - sign
    has_to = jnp.logical_and(pos + 2 * sign >= 0, pos + 2 * sign < half)
    has_from = jnp.logical_and(pos - 2 * sign >= 0, pos - 2 * sign < half)
    far_to = base + lax.rem(pos + half + 2 * sign, half)
    far_from = base + lax.rem(pos + half - 2 * sign, half)
    side = label + 2 - 4 * lax.rem(lax.div(label, 2), 2)

    near_slot = 2 - 2 * odd
    far_slot = 2 * odd

    def amp_copy(b):
        start, size = b * block, block
        if isinstance(b, int) and b == 0:
            start, size = 2 * chunk, block - 2 * chunk
        part_rows = pl.ds(start, size)
        return pltpu.make_async_copy(amp_hbm.at[0, 0, part_rows], amp.at[part_rows], amp_sem.at[b])

    def head_copy():
        part_rows = pl.ds(0, 2 * chunk)
        return pltpu.make_async_copy(
            amp_hbm.at[0, 0, part_rows], amp.at[part_rows], amp_sem.at[blocks]
        )

    def part_copy(b):
        part_rows = pl.ds(b * block, block)
        return pltpu.make_async_copy(part_hbm.at[0, 0, part_rows], part.at[part_rows], part_sem.at[b])

    def hole_copy(slot):
        return pltpu.make_async_copy(hole_hbm.at[0, 0, slot], hole.at[slot], hole_sem.at[slot])

    head_copy().start()

    @pl.when(has_to)
    def _():
        hole_copy(far_slot).start()

    hole_copy(near_slot).start()
    for b in range(blocks):
        amp_copy(b).start()
        part_copy(b).start()
    hole_copy(1).start()

    barrier = pltpu.get_barrier_semaphore()
    pl.semaphore_signal(barrier, inc=1, device_id={"ja": near}, device_id_type=MESH)
    pl.semaphore_signal(barrier, inc=1, device_id={"pt": side}, device_id_type=MESH)

    @pl.when(has_to)
    def _():
        pl.semaphore_signal(barrier, inc=1, device_id={"ja": far_to}, device_id_type=MESH)

    @pl.when(has_from)
    def _():
        pl.semaphore_signal(barrier, inc=1, device_id={"ja": far_from}, device_id_type=MESH)

    def weight(slot, source, valid):
        clipped = jnp.clip(source, 0, chans - 1)
        return jnp.where(valid, wts[slot, clipped], 0.0)

    def pick(when_odd, when_even, slot_odd, slot_even, valid):
        return jnp.where(
            odd == 1, weight(slot_odd, when_odd, valid), weight(slot_even, when_even, valid)
        )

    always = half > 1
    own_w = wts[1, chan]
    near_w = pick(chan, chan, 0, 2, always)
    far_w = pick(chan, chan, 2, 0, has_to)
    from_near_w = pick(near, near, 2, 0, always)
    from_next_w = pick(chan + 1, chan - 1, 0, 2, has_to)
    from_far_w = pick(chan - 2, chan + 2, 2, 0, has_from)
    live_count = live[0, 0]

    def span(first, count):
        if isinstance(first, int):
            return pl.ds(first, count)
        return pl.ds(pl.multiple_of(first, count), count)

    def at(k):
        return span(k * chunk, chunk)

    def alive(first, count, columns):
        ids = lax.broadcasted_iota(jnp.int32, (count, columns), 0) + first
        return ids < live_count

    def masked(first, count):
        vals = amp[span(first, count)]
        return jnp.where(alive(first, count, holes), vals, jnp.zeros_like(vals))

    def product(k, slot):
        return jnp.dot(amp[at(k)], hole[slot], preferred_element_type=jnp.float32)

    def remote(src, dst, send, recv, target):
        return pltpu.make_async_remote_copy(
            src_ref=src, dst_ref=dst, send_sem=send, recv_sem=recv,
            device_id=target, device_id_type=MESH,
        )

    def item(k):
        return k + 4

    def far_copy(i, where):
        return remote(far_out.at[where], far_in.at[where], far_s.at[i], far_r.at[i], {"ja": far_to})

    def near_copy(i, where):
        return remote(near_out.at[where], near_in.at[where], near_s.at[i], near_r.at[i], {"ja": near})

    def side_copy(k):
        return remote(side_out.at[at(k)], side_in.at[at(k)], side_s.at[k], side_r.at[k], {"pt": side})

    def inter_copy(m):
        return remote(inter.at[m], mix_in.at[m], inter_s.at[m], inter_r.at[m], {"pt": side})

    def raw_copy(m):
        return remote(mix_in.at[m], raw_in.at[m], raw_s.at[m], raw_r.at[m], {"ja": near})

    def fwd_copy(m):
        return remote(raw_in.at[m], fwd_in.at[m], fwd_s.at[m], fwd_r.at[m], {"ja": far_from})

    def cfar_copy(m):
        return remote(mix_in.at[raw + m], cfar_in.at[m], cfar_s.at[m], cfar_r.at[m], {"ja": far_to})

    def cnear_copy(m):
        return remote(cnear_out.at[m], cnear_in.at[m], cnear_s.at[m], cnear_r.at[m], {"ja": near})

    def sub_span(i):
        return pl.ds(*subs[i])

    def chunk_copies(make, k):
        if isinstance(k, int) and k in first_items:
            return [make(i, sub_span(i)) for i in first_items[k]]
        return [make(item(k), at(k))]

    def send_far(k):
        far_out[at(k)] = (far_w * product(k, far_slot)).astype(jnp.bfloat16)
        for copy in chunk_copies(far_copy, k):
            copy.start()

    def send_near(i, where, there):
        @pl.when(has_from)
        def _():
            far_copy(i, where).wait_recv()

        @pl.when(jnp.logical_not(has_from))
        def _():
            far_in[where] = jnp.zeros((there.size, holes), jnp.bfloat16)

        value = near_p[there] + far_in[where].astype(jnp.float32)
        near_out[where] = value.astype(jnp.bfloat16)
        near_copy(i, where).start()

    def send_near_sub(i):
        send_near(i, sub_span(i), sub_span(i))

    def send_side(k):
        side_p[...] = own_w * product(k, 1)
        for copy in chunk_copies(near_copy, k):
            copy.wait_recv()
        value = side_p[...] + near_in[at(k)].astype(jnp.float32)
        side_out[at(k)] = value.astype(jnp.bfloat16)
        side_copy(k).start()

    def finish(first, count, low, high):
        where = span(first, count)
        value = jnp.dot(amp[where], mix[:, low:high], preferred_element_type=jnp.float32)
        value = value + side_in[where, low:high].astype(jnp.float32)
        value = jnp.where(alive(first, count, high - low), value, jnp.zeros_like(value))
        out[0, 0, where, low:high] = value.astype(jnp.bfloat16)

    head_copy().wait()
    amp[pl.ds(0, 2 * chunk)] = masked(0, 2 * chunk)

    @pl.when(has_to)
    def _():
        hole_copy(far_slot).wait()

    pl.semaphore_wait(barrier, 2 + has_to.astype(jnp.int32) + has_from.astype(jnp.int32))

    @pl.when(has_to)
    def _():
        send_far(0)
        send_far(1)

    hole_copy(near_slot).wait()
    for k in range(2):
        near_p[at(k)] = near_w * product(k, near_slot)

    def late_far(k):
        @pl.when(has_to)
        def _():
            send_far(k)

    def gather(b):
        amp_copy(b).wait()
        part_copy(b).wait()
        value = masked(b * block, block)
        amp[span(b * block, block)] = value
        value = lax.dot_general(
            value, part[span(b * block, block)],
            (((0,), (0,)), ((), ())), preferred_element_type=jnp.float32,
        )
        acc[...] = value if b == 0 else acc[...] + value

    between = {0: (), 1: (), 2: (0, 1), 3: (2, 3), 4: (4,)}
    for b in range(blocks):
        gather(b)
        for i in between.get(b, ()):
            send_near_sub(i)
        if b < 3:
            late_far(2 + b)

    for m in range(mixes):
        inter[m] = acc[:, m * width:(m + 1) * width].astype(jnp.bfloat16)
        inter_copy(m).start()
    sent = {i for b in range(blocks) for i in between.get(b, ())}
    for i in range(len(subs)):
        if i not in sent:
            send_near_sub(i)
    hole_copy(1).wait()

    def step(t, far=True, finishing=False):
        if far:
            late_far(t + HEAD)
        near_p[:chunk] = near_w * product(t, near_slot)
        send_near(item(t), at(t), pl.ds(0, chunk))
        send_side(t - GAP)
        if finishing:
            k = t - LAG
            side_copy(k).wait_recv()
            finish(k * chunk, chunk, 0, wide)

    for m in range(raw):
        inter_copy(m).wait_recv()
        raw_copy(m).start()
    step(2)
    step(3)
    for m in range(raw):
        raw_copy(m).wait_recv()

        @pl.when(has_from)
        def _():
            fwd_copy(m).start()

    for m in range(raw, mixes):
        inter_copy(m).wait_recv()

    pl.loop(4, LAG)(step)

    for m in range(raw):
        @pl.when(has_to)
        def _():
            fwd_copy(m).wait_recv()

        @pl.when(jnp.logical_not(has_to))
        def _():
            fwd_in[m] = jnp.zeros((holes, width), jnp.bfloat16)

        value = own_w * mix_in[m].astype(jnp.float32)
        value = value + from_near_w * raw_in[m].astype(jnp.float32)
        value = value + from_next_w * fwd_in[m].astype(jnp.float32)
        mix[:, m * width:(m + 1) * width] = value.astype(jnp.bfloat16)

    pl.loop(LAG, terms - HEAD)(functools.partial(step, finishing=True))

    for m in range(tail):
        @pl.when(has_to)
        def _():
            cfar_copy(m).start()

    pl.loop(terms - HEAD, terms)(functools.partial(step, far=False, finishing=True))

    for m in range(tail):
        @pl.when(has_from)
        def _():
            cfar_copy(m).wait_recv()

        @pl.when(jnp.logical_not(has_from))
        def _():
            cfar_in[m] = jnp.zeros((holes, width), jnp.bfloat16)

        value = near_w * mix_in[raw + m].astype(jnp.float32)
        value = value + from_far_w * cfar_in[m].astype(jnp.float32)
        cnear_out[m] = value.astype(jnp.bfloat16)
        cnear_copy(m).start()

    for k in range(terms - GAP, terms):
        send_side(k)

    def finish_chunk(k):
        side_copy(k).wait_recv()
        finish(k * chunk, chunk, 0, wide)

    pl.loop(terms - LAG, terms - 2)(finish_chunk)

    for m in range(tail):
        low = wide + m * width
        high = low + width
        cnear_copy(m).wait_recv()
        value = own_w * mix_in[raw + m].astype(jnp.float32) + cnear_in[m].astype(jnp.float32)
        mix[:, low:high] = value.astype(jnp.bfloat16)

        @pl.loop(0, blocks - 1)
        def _(b):
            finish(b * block, block, low, high)

        if m == 0:
            finish_chunk(terms - 2)

            @pl.when(has_to)
            def _():
                for k in range(2):
                    for copy in chunk_copies(far_copy, k):
                        copy.wait_send()

                @pl.loop(2, terms)
                def _(k):
                    far_copy(item(k), at(k)).wait_send()

                for n in range(tail):
                    cfar_copy(n).wait_send()

            @pl.when(has_from)
            def _():
                for n in range(raw):
                    fwd_copy(n).wait_send()

            for n in range(mixes):
                inter_copy(n).wait_send()
            for n in range(raw):
                raw_copy(n).wait_send()

    finish_chunk(terms - 1)
    finish((blocks - 1) * block, block, wide, holes)

    for k in range(2):
        for copy in chunk_copies(near_copy, k):
            copy.wait_send()

    @pl.loop(2, terms)
    def _(k):
        near_copy(item(k), at(k)).wait_send()

    @pl.loop(0, terms)
    def _(k):
        side_copy(k).wait_send()

    for n in range(tail):
        cnear_copy(n).wait_send()


def shards(half, amplitudes, live_rows, hole_coupling, part_hole, recoupling):
    rows, holes = amplitudes.shape[2:]
    chunk, block = min(CHUNK, holes), min(BLOCK, rows)
    width = min(128, holes)
    mixes = holes // width
    raw = mixes // 2
    tail = mixes - raw
    terms = rows // chunk
    bf = jnp.bfloat16
    stream = pltpu.VMEM((rows, holes), bf)

    def panels(count):
        return pltpu.VMEM((count, holes, width), bf)

    sems = pltpu.SemaphoreType.DMA
    flops = 10 * rows * holes * holes
    return pl.pallas_call(
        functools.partial(kernel, half, chunk, block, raw),
        out_shape=pltpu.VMEM(amplitudes.shape, bf),
        in_specs=[pl.BlockSpec(memory_space=pltpu.SMEM)] * 2
        + [pl.BlockSpec(memory_space=pl.ANY)] * 3,
        out_specs=pl.BlockSpec(memory_space=pltpu.VMEM),
        scratch_shapes=[
            pltpu.VMEM((rows, holes), bf),
            pltpu.VMEM((3, holes, holes), bf),
            pltpu.VMEM((rows, holes), bf),
            pltpu.VMEM((holes, holes), jnp.float32),
            panels(mixes), panels(mixes), panels(raw), panels(raw),
            panels(tail), panels(tail), panels(tail),
            pltpu.VMEM((holes, holes), bf),
            stream, stream, stream, stream, stream, stream,
            pltpu.VMEM((2 * chunk, holes), jnp.float32),
            pltpu.VMEM((chunk, holes), jnp.float32),
            sems((rows // block + 1,)),
            sems((rows // block,)),
            sems((3,)),
            sems((terms + 4,)), sems((terms + 4,)), sems((terms + 4,)), sems((terms + 4,)),
            sems((terms,)), sems((terms,)),
            sems((mixes,)), sems((mixes,)),
            sems((raw,)), sems((raw,)), sems((raw,)), sems((raw,)),
            sems((tail,)), sems((tail,)), sems((tail,)), sems((tail,)),
        ],
        compiler_params=pltpu.CompilerParams(
            collective_id=0, has_side_effects=True, vmem_limit_bytes=60 << 20
        ),
        cost_estimate=pl.CostEstimate(
            flops=flops, bytes_accessed=6 * rows * holes * 2, transcendentals=0
        ),
        name="gt_bar",
    )(recoupling.T, live_rows, amplitudes, hole_coupling, part_hole)


def solution(mesh):
    in_specs = (
        P("ja", "pt", None, None),
        P("ja", "pt"),
        P("ja", "pt", None, None, None),
        P("ja", "pt", None, None),
        P(),
    )
    out_specs = P("ja", "pt", None, None)
    body = functools.partial(shards, mesh.shape["ja"] // 2)
    return jax.shard_map(body, mesh=mesh, in_specs=in_specs, out_specs=out_specs, check_vma=False)
```

```python
import functools

import jax
import jax.numpy as jnp
from jax import lax
from jax.experimental import pallas as pl
from jax.experimental.pallas import tpu as pltpu
from jax.sharding import PartitionSpec as P

MESH = pl.DeviceIdType.MESH
CHUNK = 128
BLOCK = 512
GATHER = 1024
HEAD = 3
GAP = 2
LAG = 9


def kernel(
    half, chunk, block, gather_rows, raw,
    wts, live, amp_hbm, hole_hbm, part_hbm, out,
    amp, hole, part, acc, inter, mix_in, raw_in, fwd_in, cfar_in, cnear_out, cnear_in, mix,
    far_out, far_in, near_out, near_in, side_out, side_in, near_p, side_p,
    amp_sem, part_sem, hole_sem,
    far_s, far_r, near_s, near_r, side_s, side_r, inter_s, inter_r,
    raw_s, raw_r, fwd_s, fwd_r, cfar_s, cfar_r, cnear_s, cnear_r,
):
    rows, holes = amp.shape
    terms = rows // chunk
    blocks = rows // block
    gathers = rows // gather_rows
    mixes, _, width = inter.shape
    tail = mixes - raw
    wide = raw * width
    quarter, mid = chunk // 4, chunk // 2
    subs = [(i * quarter, quarter) for i in range(4)] + [(chunk + i * mid, mid) for i in range(2)]
    first_items = {0: range(0, 4), 1: range(4, 6)}

    chans = wts.shape[1]
    chan = lax.axis_index("ja")
    label = lax.axis_index("pt")
    pos = lax.rem(chan, half)
    base = chan - pos
    odd = lax.rem(chan, 2)
    sign = 2 * odd - 1
    near = chan - sign
    has_to = jnp.logical_and(pos + 2 * sign >= 0, pos + 2 * sign < half)
    has_from = jnp.logical_and(pos - 2 * sign >= 0, pos - 2 * sign < half)
    far_to = base + lax.rem(pos + half + 2 * sign, half)
    far_from = base + lax.rem(pos + half - 2 * sign, half)
    side = label + 2 - 4 * lax.rem(lax.div(label, 2), 2)

    near_slot = 2 - 2 * odd
    far_slot = 2 * odd

    def amp_copy(b):
        start, size = b * gather_rows, gather_rows
        if b == 0:
            start, size = 2 * chunk, gather_rows - 2 * chunk
        part_rows = pl.ds(start, size)
        return pltpu.make_async_copy(amp_hbm.at[0, 0, part_rows], amp.at[part_rows], amp_sem.at[b])

    def head_copy():
        part_rows = pl.ds(0, 2 * chunk)
        return pltpu.make_async_copy(
            amp_hbm.at[0, 0, part_rows], amp.at[part_rows], amp_sem.at[gathers]
        )

    def part_copy(b):
        part_rows = pl.ds(b * gather_rows, gather_rows)
        return pltpu.make_async_copy(part_hbm.at[0, 0, part_rows], part.at[part_rows], part_sem.at[b])

    def hole_copy(slot):
        return pltpu.make_async_copy(hole_hbm.at[0, 0, slot], hole.at[slot], hole_sem.at[slot])

    head_copy().start()

    @pl.when(has_to)
    def _():
        hole_copy(far_slot).start()

    hole_copy(near_slot).start()
    for b in range(gathers):
        amp_copy(b).start()
        part_copy(b).start()
    hole_copy(1).start()

    barrier = pltpu.get_barrier_semaphore()
    pl.semaphore_signal(barrier, inc=1, device_id={"ja": near}, device_id_type=MESH)
    pl.semaphore_signal(barrier, inc=1, device_id={"pt": side}, device_id_type=MESH)

    @pl.when(has_to)
    def _():
        pl.semaphore_signal(barrier, inc=1, device_id={"ja": far_to}, device_id_type=MESH)

    @pl.when(has_from)
    def _():
        pl.semaphore_signal(barrier, inc=1, device_id={"ja": far_from}, device_id_type=MESH)

    def weight(slot, source, valid):
        clipped = jnp.clip(source, 0, chans - 1)
        return jnp.where(valid, wts[slot, clipped], 0.0)

    def pick(when_odd, when_even, slot_odd, slot_even, valid):
        return jnp.where(
            odd == 1, weight(slot_odd, when_odd, valid), weight(slot_even, when_even, valid)
        )

    always = half > 1
    own_w = wts[1, chan]
    near_w = pick(chan, chan, 0, 2, always)
    far_w = pick(chan, chan, 2, 0, has_to)
    from_near_w = pick(near, near, 2, 0, always)
    from_next_w = pick(chan + 1, chan - 1, 0, 2, has_to)
    from_far_w = pick(chan - 2, chan + 2, 2, 0, has_from)
    live_count = live[0, 0]

    def span(first, count):
        if isinstance(first, int):
            return pl.ds(first, count)
        return pl.ds(pl.multiple_of(first, count), count)

    def at(k):
        return span(k * chunk, chunk)

    def alive(first, count, columns):
        ids = lax.broadcasted_iota(jnp.int32, (count, columns), 0) + first
        return ids < live_count

    def masked(first, count):
        return amp[span(first, count)] * alive(first, count, 1).astype(jnp.bfloat16)

    def product(k, slot):
        return jnp.dot(amp[at(k)], hole[slot], preferred_element_type=jnp.float32)

    def remote(src, dst, send, recv, target):
        return pltpu.make_async_remote_copy(
            src_ref=src, dst_ref=dst, send_sem=send, recv_sem=recv,
            device_id=target, device_id_type=MESH,
        )

    def item(k):
        return k + 4

    def far_copy(i, where):
        return remote(far_out.at[where], far_in.at[where], far_s.at[i], far_r.at[i], {"ja": far_to})

    def near_copy(i, where):
        return remote(near_out.at[where], near_in.at[where], near_s.at[i], near_r.at[i], {"ja": near})

    def side_copy(k):
        return remote(side_out.at[at(k)], side_in.at[at(k)], side_s.at[k], side_r.at[k], {"pt": side})

    def inter_copy(m):
        return remote(inter.at[m], mix_in.at[m], inter_s.at[m], inter_r.at[m], {"pt": side})

    def raw_copy(m):
        return remote(mix_in.at[m], raw_in.at[m], raw_s.at[m], raw_r.at[m], {"ja": near})

    def fwd_copy(m):
        return remote(raw_in.at[m], fwd_in.at[m], fwd_s.at[m], fwd_r.at[m], {"ja": far_from})

    def cfar_copy(m):
        return remote(mix_in.at[raw + m], cfar_in.at[m], cfar_s.at[m], cfar_r.at[m], {"ja": far_to})

    def cnear_copy(m):
        return remote(cnear_out.at[m], cnear_in.at[m], cnear_s.at[m], cnear_r.at[m], {"ja": near})

    def sub_span(i):
        return pl.ds(*subs[i])

    def chunk_copies(make, k):
        if isinstance(k, int) and k in first_items:
            return [make(i, sub_span(i)) for i in first_items[k]]
        return [make(item(k), at(k))]

    def send_far(k):
        far_out[at(k)] = (far_w * product(k, far_slot)).astype(jnp.bfloat16)
        for copy in chunk_copies(far_copy, k):
            copy.start()

    def send_near(i, where, there):
        @pl.when(has_from)
        def _():
            far_copy(i, where).wait_recv()

        @pl.when(jnp.logical_not(has_from))
        def _():
            far_in[where] = jnp.zeros((there.size, holes), jnp.bfloat16)

        value = near_p[there] + far_in[where].astype(jnp.float32)
        near_out[where] = value.astype(jnp.bfloat16)
        near_copy(i, where).start()

    def send_side(k):
        side_p[...] = own_w * product(k, 1)
        for copy in chunk_copies(near_copy, k):
            copy.wait_recv()
        value = side_p[...] + near_in[at(k)].astype(jnp.float32)
        side_out[at(k)] = value.astype(jnp.bfloat16)
        side_copy(k).start()

    def finish(first, count, low, high):
        where = span(first, count)
        value = jnp.dot(amp[where], mix[:, low:high], preferred_element_type=jnp.float32)
        value = value + side_in[where, low:high].astype(jnp.float32)
        value = jnp.where(alive(first, count, high - low), value, jnp.zeros_like(value))
        out[0, 0, where, low:high] = value.astype(jnp.bfloat16)

    head_copy().wait()
    amp[pl.ds(0, 2 * chunk)] = masked(0, 2 * chunk)

    @pl.when(has_to)
    def _():
        hole_copy(far_slot).wait()

    pl.semaphore_wait(barrier, 2 + has_to.astype(jnp.int32) + has_from.astype(jnp.int32))

    @pl.when(has_to)
    def _():
        send_far(0)
        send_far(1)

    hole_copy(near_slot).wait()
    for k in range(2):
        near_p[at(k)] = near_w * product(k, near_slot)

    @pl.when(jnp.logical_not(has_from))
    def _():
        for i in range(len(subs)):
            where = sub_span(i)
            near_out[where] = near_p[where].astype(jnp.bfloat16)
            near_copy(i, where).start()

    def late_far(k):
        @pl.when(has_to)
        def _():
            send_far(k)

    for b in range(gathers):
        amp_copy(b).wait()
        part_copy(b).wait()
        where = pl.ds(b * gather_rows, gather_rows)
        value = masked(b * gather_rows, gather_rows)
        amp[where] = value
        value = lax.dot_general(
            value, part[where], (((0,), (0,)), ((), ())), preferred_element_type=jnp.float32,
        )
        if b:
            value = acc[...] + value
        if b < gathers - 1:
            acc[...] = value
            continue
        for m in range(mixes):
            inter[m] = value[:, m * width:(m + 1) * width].astype(jnp.bfloat16)
            inter_copy(m).start()

    early = {1: (2,), 3: (3,), 4: (4,)}
    for i in range(len(subs)):
        @pl.when(has_from)
        def _():
            where = sub_span(i)
            far_copy(i, where).wait_recv()
            value = near_p[where] + far_in[where].astype(jnp.float32)
            near_out[where] = value.astype(jnp.bfloat16)
            near_copy(i, where).start()

        for k in early.get(i, ()):
            late_far(k)
    hole_copy(1).wait()

    def step(t, far=True, finishing=False):
        if far:
            late_far(t + HEAD)
        near_p[:chunk] = near_w * product(t, near_slot)
        send_near(item(t), at(t), pl.ds(0, chunk))
        send_side(t - GAP)
        if finishing:
            k = t - LAG
            side_copy(k).wait_recv()
            finish(k * chunk, chunk, 0, wide)

    for m in range(raw):
        inter_copy(m).wait_recv()
        raw_copy(m).start()
    step(2)
    step(3)
    for m in range(raw):
        raw_copy(m).wait_recv()

        @pl.when(has_from)
        def _():
            fwd_copy(m).start()

    for m in range(raw, mixes):
        inter_copy(m).wait_recv()

    pl.loop(4, LAG)(step)

    for m in range(raw):
        @pl.when(has_to)
        def _():
            fwd_copy(m).wait_recv()

        @pl.when(jnp.logical_not(has_to))
        def _():
            fwd_in[m] = jnp.zeros((holes, width), jnp.bfloat16)

        value = own_w * mix_in[m].astype(jnp.float32)
        value = value + from_near_w * raw_in[m].astype(jnp.float32)
        value = value + from_next_w * fwd_in[m].astype(jnp.float32)
        mix[:, m * width:(m + 1) * width] = value.astype(jnp.bfloat16)

    pl.loop(LAG, terms - HEAD)(functools.partial(step, finishing=True))

    for m in range(tail):
        @pl.when(has_to)
        def _():
            cfar_copy(m).start()

    pl.loop(terms - HEAD, terms)(functools.partial(step, far=False, finishing=True))

    for m in range(tail):
        @pl.when(has_from)
        def _():
            cfar_copy(m).wait_recv()

        @pl.when(jnp.logical_not(has_from))
        def _():
            cfar_in[m] = jnp.zeros((holes, width), jnp.bfloat16)

        value = near_w * mix_in[raw + m].astype(jnp.float32)
        value = value + from_far_w * cfar_in[m].astype(jnp.float32)
        cnear_out[m] = value.astype(jnp.bfloat16)
        cnear_copy(m).start()

    for k in range(terms - GAP, terms):
        send_side(k)

    def finish_chunk(k):
        side_copy(k).wait_recv()
        finish(k * chunk, chunk, 0, wide)

    pl.loop(terms - LAG, terms - 2)(finish_chunk)

    for m in range(tail):
        low = wide + m * width
        high = low + width
        cnear_copy(m).wait_recv()
        value = own_w * mix_in[raw + m].astype(jnp.float32) + cnear_in[m].astype(jnp.float32)
        mix[:, low:high] = value.astype(jnp.bfloat16)

        @pl.loop(0, blocks - 1)
        def _(b):
            finish(b * block, block, low, high)

        if m == 0:
            finish_chunk(terms - 2)

            @pl.when(has_to)
            def _():
                for k in range(2):
                    for copy in chunk_copies(far_copy, k):
                        copy.wait_send()

                @pl.loop(2, terms)
                def _(k):
                    far_copy(item(k), at(k)).wait_send()

                for n in range(tail):
                    cfar_copy(n).wait_send()

            @pl.when(has_from)
            def _():
                for n in range(raw):
                    fwd_copy(n).wait_send()

            for n in range(mixes):
                inter_copy(n).wait_send()
            for n in range(raw):
                raw_copy(n).wait_send()

    finish_chunk(terms - 1)
    finish((blocks - 1) * block, block, wide, holes)

    for k in range(2):
        for copy in chunk_copies(near_copy, k):
            copy.wait_send()

    @pl.loop(2, terms)
    def _(k):
        near_copy(item(k), at(k)).wait_send()

    @pl.loop(0, terms)
    def _(k):
        side_copy(k).wait_send()

    for n in range(tail):
        cnear_copy(n).wait_send()


def shards(half, amplitudes, live_rows, hole_coupling, part_hole, recoupling):
    rows, holes = amplitudes.shape[2:]
    chunk, block = min(CHUNK, holes), min(BLOCK, rows)
    gather = min(GATHER, rows)
    width = min(128, holes)
    mixes = holes // width
    raw = mixes // 2
    tail = mixes - raw
    terms = rows // chunk
    bf = jnp.bfloat16
    stream = pltpu.VMEM((rows, holes), bf)

    def panels(count):
        return pltpu.VMEM((count, holes, width), bf)

    sems = pltpu.SemaphoreType.DMA
    flops = 10 * rows * holes * holes
    return pl.pallas_call(
        functools.partial(kernel, half, chunk, block, gather, raw),
        out_shape=pltpu.VMEM(amplitudes.shape, bf),
        in_specs=[pl.BlockSpec(memory_space=pltpu.SMEM)] * 2
        + [pl.BlockSpec(memory_space=pl.ANY)] * 3,
        out_specs=pl.BlockSpec(memory_space=pltpu.VMEM),
        scratch_shapes=[
            pltpu.VMEM((rows, holes), bf),
            pltpu.VMEM((3, holes, holes), bf),
            pltpu.VMEM((rows, holes), bf),
            pltpu.VMEM((holes, holes), jnp.float32),
            panels(mixes), panels(mixes), panels(raw), panels(raw),
            panels(tail), panels(tail), panels(tail),
            pltpu.VMEM((holes, holes), bf),
            stream, stream, stream, stream, stream, stream,
            pltpu.VMEM((2 * chunk, holes), jnp.float32),
            pltpu.VMEM((chunk, holes), jnp.float32),
            sems((rows // gather + 1,)),
            sems((rows // gather,)),
            sems((3,)),
            sems((terms + 4,)), sems((terms + 4,)), sems((terms + 4,)), sems((terms + 4,)),
            sems((terms,)), sems((terms,)),
            sems((mixes,)), sems((mixes,)),
            sems((raw,)), sems((raw,)), sems((raw,)), sems((raw,)),
            sems((tail,)), sems((tail,)), sems((tail,)), sems((tail,)),
        ],
        compiler_params=pltpu.CompilerParams(
            collective_id=0, has_side_effects=True, vmem_limit_bytes=60 << 20
        ),
        cost_estimate=pl.CostEstimate(
            flops=flops, bytes_accessed=6 * rows * holes * 2, transcendentals=0
        ),
        name="gt_bar",
    )(recoupling.T, live_rows, amplitudes, hole_coupling, part_hole)


def solution(mesh):
    in_specs = (
        P("ja", "pt", None, None),
        P("ja", "pt"),
        P("ja", "pt", None, None, None),
        P("ja", "pt", None, None),
        P(),
    )
    out_specs = P("ja", "pt", None, None)
    body = functools.partial(shards, mesh.shape["ja"] // 2)
    return jax.shard_map(body, mesh=mesh, in_specs=in_specs, out_specs=out_specs, check_vma=False)
```

```python
import functools

import jax
import jax.numpy as jnp
from jax import lax
from jax.experimental import pallas as pl
from jax.experimental.pallas import tpu as pltpu
from jax.sharding import PartitionSpec as P

MESH = pl.DeviceIdType.MESH
CHUNK = 128
BLOCK = 512
GATHER = 1024
HEAD = 3
GAP = 2
LAG = 9
SWEEPS = 1


def kernel(
    half, chunk, block, gather_rows, raw,
    wts, live, amp_hbm, hole_hbm, part_hbm, out,
    amp, hole, part, acc, inter, mix_in, raw_in, fwd_in, cfar_in, cnear_out, cnear_in, mix,
    ext_in, next_in,
    far_out, far_in, near_out, near_in, side_out, side_in, near_p, side_p,
    amp_sem, part_sem, hole_sem,
    far_s, far_r, near_s, near_r, side_s, side_r, inter_s, inter_r,
    raw_s, raw_r, fwd_s, fwd_r, cfar_s, cfar_r, cnear_s, cnear_r,
    ext_s, ext_r, next_s, next_r,
):
    rows, holes = amp.shape
    terms = rows // chunk
    blocks = rows // block
    gathers = rows // gather_rows
    mixes, _, width = inter.shape
    tail = mixes - raw
    wide = raw * width
    quarter, mid = chunk // 4, chunk // 2
    subs = [
        (0, mid), (mid, quarter), (mid + quarter, quarter), (chunk, mid), (chunk + mid, mid)
    ]
    first_items = {0: range(0, 3), 1: range(3, 5)}
    ahead = len(subs) - 2
    direct = pl.ds(0, mid)

    chans = wts.shape[1]
    chan = lax.axis_index("ja")
    label = lax.axis_index("pt")
    pos = lax.rem(chan, half)
    base = chan - pos
    odd = lax.rem(chan, 2)
    sign = 2 * odd - 1
    near = chan - sign
    has_to = jnp.logical_and(pos + 2 * sign >= 0, pos + 2 * sign < half)
    has_from = jnp.logical_and(pos - 2 * sign >= 0, pos - 2 * sign < half)
    far_to = base + lax.rem(pos + half + 2 * sign, half)
    far_from = base + lax.rem(pos + half - 2 * sign, half)
    side = label + 2 - 4 * lax.rem(lax.div(label, 2), 2)

    near_slot = 2 - 2 * odd
    far_slot = 2 * odd

    def amp_copy(b):
        start, size = b * gather_rows, gather_rows
        if b == 0:
            start, size = 2 * chunk, gather_rows - 2 * chunk
        part_rows = pl.ds(start, size)
        return pltpu.make_async_copy(amp_hbm.at[0, 0, part_rows], amp.at[part_rows], amp_sem.at[b])

    def head_copy():
        part_rows = pl.ds(0, 2 * chunk)
        return pltpu.make_async_copy(
            amp_hbm.at[0, 0, part_rows], amp.at[part_rows], amp_sem.at[gathers]
        )

    def part_copy(b):
        part_rows = pl.ds(b * gather_rows, gather_rows)
        return pltpu.make_async_copy(part_hbm.at[0, 0, part_rows], part.at[part_rows], part_sem.at[b])

    def hole_copy(slot):
        return pltpu.make_async_copy(hole_hbm.at[0, 0, slot], hole.at[slot], hole_sem.at[slot])

    head_copy().start()

    @pl.when(has_to)
    def _():
        hole_copy(far_slot).start()

    hole_copy(near_slot).start()
    for b in range(gathers):
        amp_copy(b).start()
        part_copy(b).start()
    hole_copy(1).start()

    barrier = pltpu.get_barrier_semaphore()
    pl.semaphore_signal(barrier, inc=1, device_id={"ja": near}, device_id_type=MESH)
    pl.semaphore_signal(barrier, inc=1, device_id={"pt": side}, device_id_type=MESH)

    @pl.when(has_to)
    def _():
        pl.semaphore_signal(barrier, inc=1, device_id={"ja": far_to}, device_id_type=MESH)

    @pl.when(has_from)
    def _():
        pl.semaphore_signal(barrier, inc=1, device_id={"ja": far_from}, device_id_type=MESH)

    def weight(slot, source, valid):
        clipped = jnp.clip(source, 0, chans - 1)
        return jnp.where(valid, wts[slot, clipped], 0.0)

    def pick(when_odd, when_even, slot_odd, slot_even, valid):
        return jnp.where(
            odd == 1, weight(slot_odd, when_odd, valid), weight(slot_even, when_even, valid)
        )

    always = half > 1
    own_w = wts[1, chan]
    near_w = pick(chan, chan, 0, 2, always)
    far_w = pick(chan, chan, 2, 0, has_to)
    from_near_w = pick(near, near, 2, 0, always)
    from_next_w = pick(chan + 1, chan - 1, 0, 2, has_to)
    from_far_w = pick(chan - 2, chan + 2, 2, 0, has_from)
    live_count = live[0, 0]

    def span(first, count):
        if isinstance(first, int):
            return pl.ds(first, count)
        return pl.ds(pl.multiple_of(first, count), count)

    def at(k):
        return span(k * chunk, chunk)

    def alive(first, count, columns):
        ids = lax.broadcasted_iota(jnp.int32, (count, columns), 0) + first
        return ids < live_count

    def masked(first, count):
        return amp[span(first, count)] * alive(first, count, 1).astype(jnp.bfloat16)

    def product(k, slot):
        return jnp.dot(amp[at(k)], hole[slot], preferred_element_type=jnp.float32)

    def remote(src, dst, send, recv, target):
        return pltpu.make_async_remote_copy(
            src_ref=src, dst_ref=dst, send_sem=send, recv_sem=recv,
            device_id=target, device_id_type=MESH,
        )

    def item(k):
        return k + ahead

    def far_copy(i, where):
        return remote(far_out.at[where], far_in.at[where], far_s.at[i], far_r.at[i], {"ja": far_to})

    def near_copy(i, where):
        return remote(near_out.at[where], near_in.at[where], near_s.at[i], near_r.at[i], {"ja": near})

    def side_copy(k):
        return remote(side_out.at[at(k)], side_in.at[at(k)], side_s.at[k], side_r.at[k], {"pt": side})

    def inter_copy(m):
        return remote(inter.at[m], mix_in.at[m], inter_s.at[m], inter_r.at[m], {"pt": side})

    def raw_copy(m):
        return remote(mix_in.at[m], raw_in.at[m], raw_s.at[m], raw_r.at[m], {"ja": near})

    def fwd_copy(m):
        return remote(raw_in.at[m], fwd_in.at[m], fwd_s.at[m], fwd_r.at[m], {"ja": far_from})

    def cfar_copy(m):
        return remote(mix_in.at[raw + m], cfar_in.at[m], cfar_s.at[m], cfar_r.at[m], {"ja": far_to})

    def cnear_copy(m):
        return remote(cnear_out.at[m], cnear_in.at[m], cnear_s.at[m], cnear_r.at[m], {"ja": near})

    def ext_copy():
        return remote(far_out.at[direct], ext_in, ext_s.at[0], ext_r.at[0], {"ja": near})

    def next_copy():
        return remote(ext_in, next_in, next_s.at[0], next_r.at[0], {"ja": far_from})

    def sub_span(i):
        return pl.ds(*subs[i])

    def chunk_copies(make, k):
        if isinstance(k, int) and k in first_items:
            lowest = 1 if make is far_copy else 0
            return [make(i, sub_span(i)) for i in first_items[k] if i >= lowest]
        return [make(item(k), at(k))]

    def send_far(k):
        far_out[at(k)] = (far_w * product(k, far_slot)).astype(jnp.bfloat16)
        for copy in chunk_copies(far_copy, k):
            copy.start()

    def send_near(i, where, there):
        @pl.when(has_from)
        def _():
            far_copy(i, where).wait_recv()

        @pl.when(jnp.logical_not(has_from))
        def _():
            far_in[where] = jnp.zeros((there.size, holes), jnp.bfloat16)

        value = near_p[there] + far_in[where].astype(jnp.float32)
        near_out[where] = value.astype(jnp.bfloat16)
        near_copy(i, where).start()

    def send_side(k):
        side_p[...] = own_w * product(k, 1)
        if isinstance(k, int) and k == 0:
            @pl.when(has_to)
            def _():
                next_copy().wait_recv()
                side_p[direct] = side_p[direct] + next_in[...].astype(jnp.float32)

        for copy in chunk_copies(near_copy, k):
            copy.wait_recv()
        value = side_p[...] + near_in[at(k)].astype(jnp.float32)
        side_out[at(k)] = value.astype(jnp.bfloat16)
        side_copy(k).start()

    def finish(first, count, low, high):
        where = span(first, count)
        value = jnp.dot(amp[where], mix[:, low:high], preferred_element_type=jnp.float32)
        value = value + side_in[where, low:high].astype(jnp.float32)
        value = jnp.where(alive(first, count, high - low), value, jnp.zeros_like(value))
        out[0, 0, where, low:high] = value.astype(jnp.bfloat16)

    head_copy().wait()
    amp[pl.ds(0, 2 * chunk)] = masked(0, 2 * chunk)

    @pl.when(has_to)
    def _():
        hole_copy(far_slot).wait()

    pl.semaphore_wait(barrier, 2 + has_to.astype(jnp.int32) + has_from.astype(jnp.int32))

    @pl.when(has_to)
    def _():
        send_far(0)
        send_far(1)

    hole_copy(near_slot).wait()
    for k in range(2):
        near_p[at(k)] = near_w * product(k, near_slot)

    near_out[direct] = near_p[direct].astype(jnp.bfloat16)
    near_copy(0, direct).start()

    @pl.when(has_to)
    def _():
        ext_copy().start()

    @pl.when(jnp.logical_not(has_from))
    def _():
        for i in range(1, len(subs)):
            where = sub_span(i)
            near_out[where] = near_p[where].astype(jnp.bfloat16)
            near_copy(i, where).start()

    def late_far(k):
        @pl.when(has_to)
        def _():
            send_far(k)

    for b in range(gathers):
        amp_copy(b).wait()
        part_copy(b).wait()
        where = pl.ds(b * gather_rows, gather_rows)
        value = masked(b * gather_rows, gather_rows)
        amp[where] = value
        value = lax.dot_general(
            value, part[where], (((0,), (0,)), ((), ())), preferred_element_type=jnp.float32,
        )
        if b:
            value = acc[...] + value
        if b < gathers - 1:
            acc[...] = value
            continue
        for m in range(mixes):
            inter[m] = value[:, m * width:(m + 1) * width].astype(jnp.bfloat16)
            inter_copy(m).start()

    behind = {1: (2,), 2: (3,), 3: (4,)}
    for i in range(1, len(subs)):
        @pl.when(has_from)
        def _():
            where = sub_span(i)
            far_copy(i, where).wait_recv()
            value = near_p[where] + far_in[where].astype(jnp.float32)
            near_out[where] = value.astype(jnp.bfloat16)
            near_copy(i, where).start()

        for k in behind.get(i, ()):
            late_far(k)
    @pl.when(has_from)
    def _():
        ext_copy().wait_recv()
        next_copy().start()

    hole_copy(1).wait()

    def step(t, far=True, finishing=False):
        if far:
            late_far(t + HEAD)
        near_p[:chunk] = near_w * product(t, near_slot)
        send_near(item(t), at(t), pl.ds(0, chunk))
        send_side(t - GAP)
        if finishing:
            k = t - LAG
            side_copy(k).wait_recv()
            finish(k * chunk, chunk, 0, wide)

    for m in range(raw):
        inter_copy(m).wait_recv()
        raw_copy(m).start()
    step(2)
    step(3)
    for m in range(raw):
        raw_copy(m).wait_recv()

        @pl.when(has_from)
        def _():
            fwd_copy(m).start()

    for m in range(raw, mixes):
        inter_copy(m).wait_recv()

    pl.loop(4, LAG)(step)

    for m in range(raw):
        @pl.when(has_to)
        def _():
            fwd_copy(m).wait_recv()

        @pl.when(jnp.logical_not(has_to))
        def _():
            fwd_in[m] = jnp.zeros((holes, width), jnp.bfloat16)

        value = own_w * mix_in[m].astype(jnp.float32)
        value = value + from_near_w * raw_in[m].astype(jnp.float32)
        value = value + from_next_w * fwd_in[m].astype(jnp.float32)
        mix[:, m * width:(m + 1) * width] = value.astype(jnp.bfloat16)

    pl.loop(LAG, terms - HEAD)(functools.partial(step, finishing=True))

    for m in range(tail):
        @pl.when(has_to)
        def _():
            cfar_copy(m).start()

    pl.loop(terms - HEAD, terms)(functools.partial(step, far=False, finishing=True))

    for m in range(tail):
        @pl.when(has_from)
        def _():
            cfar_copy(m).wait_recv()

        @pl.when(jnp.logical_not(has_from))
        def _():
            cfar_in[m] = jnp.zeros((holes, width), jnp.bfloat16)

        value = near_w * mix_in[raw + m].astype(jnp.float32)
        value = value + from_far_w * cfar_in[m].astype(jnp.float32)
        cnear_out[m] = value.astype(jnp.bfloat16)
        cnear_copy(m).start()

    for k in range(terms - GAP, terms):
        send_side(k)

    def finish_chunk(k):
        side_copy(k).wait_recv()
        finish(k * chunk, chunk, 0, wide)

    pl.loop(terms - LAG, terms - 2)(finish_chunk)

    finish_chunk(terms - 2)

    @pl.when(has_to)
    def _():
        for k in range(2):
            for copy in chunk_copies(far_copy, k):
                copy.wait_send()

        @pl.loop(2, terms)
        def _(k):
            far_copy(item(k), at(k)).wait_send()

        for n in range(tail):
            cfar_copy(n).wait_send()
        ext_copy().wait_send()

    @pl.when(has_from)
    def _():
        for n in range(raw):
            fwd_copy(n).wait_send()
        next_copy().wait_send()

    for n in range(mixes):
        inter_copy(n).wait_send()
    for n in range(raw):
        raw_copy(n).wait_send()
    for k in range(2):
        for copy in chunk_copies(near_copy, k):
            copy.wait_send()

    @pl.loop(2, terms)
    def _(k):
        near_copy(item(k), at(k)).wait_send()

    @pl.loop(0, terms - 2)
    def _(k):
        side_copy(k).wait_send()

    for m in range(tail):
        cnear_copy(m).wait_recv()
        value = own_w * mix_in[raw + m].astype(jnp.float32) + cnear_in[m].astype(jnp.float32)
        mix[:, wide + m * width:wide + (m + 1) * width] = value.astype(jnp.bfloat16)

    for b in range(SWEEPS):
        count = (rows - chunk) // SWEEPS
        finish(b * count, count, wide, holes)

    side_copy(terms - 1).wait_recv()
    finish((terms - 1) * chunk, chunk, 0, holes)

    for k in range(terms - 2, terms):
        side_copy(k).wait_send()
    for m in range(tail):
        cnear_copy(m).wait_send()


def shards(half, amplitudes, live_rows, hole_coupling, part_hole, recoupling):
    rows, holes = amplitudes.shape[2:]
    chunk, block = min(CHUNK, holes), min(BLOCK, rows)
    gather = min(GATHER, rows)
    width = min(128, holes)
    mixes = holes // width
    raw = mixes // 2
    tail = mixes - raw
    terms = rows // chunk
    bf = jnp.bfloat16
    stream = pltpu.VMEM((rows, holes), bf)

    def panels(count):
        return pltpu.VMEM((count, holes, width), bf)

    sems = pltpu.SemaphoreType.DMA
    flops = 10 * rows * holes * holes
    return pl.pallas_call(
        functools.partial(kernel, half, chunk, block, gather, raw),
        out_shape=pltpu.VMEM(amplitudes.shape, bf),
        in_specs=[pl.BlockSpec(memory_space=pltpu.SMEM)] * 2
        + [pl.BlockSpec(memory_space=pl.ANY)] * 3,
        out_specs=pl.BlockSpec(memory_space=pltpu.VMEM),
        scratch_shapes=[
            pltpu.VMEM((rows, holes), bf),
            pltpu.VMEM((3, holes, holes), bf),
            pltpu.VMEM((rows, holes), bf),
            pltpu.VMEM((holes, holes), jnp.float32),
            panels(mixes), panels(mixes), panels(raw), panels(raw),
            panels(tail), panels(tail), panels(tail),
            pltpu.VMEM((holes, holes), bf),
            pltpu.VMEM((chunk // 2, holes), bf),
            pltpu.VMEM((chunk // 2, holes), bf),
            stream, stream, stream, stream, stream, stream,
            pltpu.VMEM((2 * chunk, holes), jnp.float32),
            pltpu.VMEM((chunk, holes), jnp.float32),
            sems((rows // gather + 1,)),
            sems((rows // gather,)),
            sems((3,)),
            sems((terms + 3,)), sems((terms + 3,)), sems((terms + 3,)), sems((terms + 3,)),
            sems((terms,)), sems((terms,)),
            sems((mixes,)), sems((mixes,)),
            sems((raw,)), sems((raw,)), sems((raw,)), sems((raw,)),
            sems((tail,)), sems((tail,)), sems((tail,)), sems((tail,)),
            sems((1,)), sems((1,)), sems((1,)), sems((1,)),
        ],
        compiler_params=pltpu.CompilerParams(
            collective_id=0, has_side_effects=True, vmem_limit_bytes=60 << 20
        ),
        cost_estimate=pl.CostEstimate(
            flops=flops, bytes_accessed=6 * rows * holes * 2, transcendentals=0
        ),
        name="gt_bar",
    )(recoupling.T, live_rows, amplitudes, hole_coupling, part_hole)


def solution(mesh):
    in_specs = (
        P("ja", "pt", None, None),
        P("ja", "pt"),
        P("ja", "pt", None, None, None),
        P("ja", "pt", None, None),
        P(),
    )
    out_specs = P("ja", "pt", None, None)
    body = functools.partial(shards, mesh.shape["ja"] // 2)
    return jax.shard_map(body, mesh=mesh, in_specs=in_specs, out_specs=out_specs, check_vma=False)
```

```python
import functools

import jax
import jax.numpy as jnp
from jax import lax
from jax.experimental import pallas as pl
from jax.experimental.pallas import tpu as pltpu
from jax.sharding import PartitionSpec as P

MESH = pl.DeviceIdType.MESH
CHUNK = 128
BLOCK = 512
GATHER = 1024
HEAD = 3
GAP = 2
LAG = 9
STEPS = 3


def kernel(
    half, chunk, block, gather_rows, raw,
    wts, live, amp_hbm, hole_hbm, part_hbm, out, amp, late,
    hole, part, acc, inter, mix_in, raw_in, fwd_in, cfar_in, cnear_out, cnear_in, mix,
    ext_in, next_in,
    far_out, far_in, near_out, near_in, side_out, side_in, near_p, side_p,
    amp_sem, part_sem, hole_sem,
    far_s, far_r, near_s, near_r, side_s, side_r, inter_s, inter_r,
    raw_s, raw_r, fwd_s, fwd_r, cfar_s, cfar_r, cnear_s, cnear_r,
    ext_s, ext_r, next_s, next_r,
):
    rows, holes = amp.shape
    terms = rows // chunk
    blocks = rows // block
    gathers = rows // gather_rows
    mixes, _, width = inter.shape
    tail = mixes - raw
    wide = raw * width
    quarter, mid = chunk // 4, chunk // 2
    subs = [
        (0, mid), (mid, quarter), (mid + quarter, quarter), (chunk, mid), (chunk + mid, mid)
    ]
    first_items = {0: range(0, 3), 1: range(3, 5)}
    ahead = len(subs) - 2
    direct = pl.ds(0, mid)

    chans = wts.shape[1]
    chan = lax.axis_index("ja")
    label = lax.axis_index("pt")
    pos = lax.rem(chan, half)
    base = chan - pos
    odd = lax.rem(chan, 2)
    sign = 2 * odd - 1
    near = chan - sign
    has_to = jnp.logical_and(pos + 2 * sign >= 0, pos + 2 * sign < half)
    has_from = jnp.logical_and(pos - 2 * sign >= 0, pos - 2 * sign < half)
    far_to = base + lax.rem(pos + half + 2 * sign, half)
    far_from = base + lax.rem(pos + half - 2 * sign, half)
    side = label + 2 - 4 * lax.rem(lax.div(label, 2), 2)

    near_slot = 2 - 2 * odd
    far_slot = 2 * odd

    def amp_copy(b):
        start, size = b * gather_rows, gather_rows
        if b == 0:
            start, size = 2 * chunk, gather_rows - 2 * chunk
        part_rows = pl.ds(start, size)
        return pltpu.make_async_copy(amp_hbm.at[0, 0, part_rows], amp.at[part_rows], amp_sem.at[b])

    def head_copy():
        part_rows = pl.ds(0, 2 * chunk)
        return pltpu.make_async_copy(
            amp_hbm.at[0, 0, part_rows], amp.at[part_rows], amp_sem.at[gathers]
        )

    def part_copy(b):
        part_rows = pl.ds(b * gather_rows, gather_rows)
        return pltpu.make_async_copy(part_hbm.at[0, 0, part_rows], part.at[part_rows], part_sem.at[b])

    def hole_copy(slot):
        return pltpu.make_async_copy(hole_hbm.at[0, 0, slot], hole.at[slot], hole_sem.at[slot])

    head_copy().start()

    @pl.when(has_to)
    def _():
        hole_copy(far_slot).start()

    hole_copy(near_slot).start()
    for b in range(gathers):
        amp_copy(b).start()
        part_copy(b).start()
    hole_copy(1).start()

    barrier = pltpu.get_barrier_semaphore()
    pl.semaphore_signal(barrier, inc=1, device_id={"ja": near}, device_id_type=MESH)
    pl.semaphore_signal(barrier, inc=1, device_id={"pt": side}, device_id_type=MESH)

    @pl.when(has_to)
    def _():
        pl.semaphore_signal(barrier, inc=1, device_id={"ja": far_to}, device_id_type=MESH)

    @pl.when(has_from)
    def _():
        pl.semaphore_signal(barrier, inc=1, device_id={"ja": far_from}, device_id_type=MESH)

    def weight(slot, source, valid):
        clipped = jnp.clip(source, 0, chans - 1)
        return jnp.where(valid, wts[slot, clipped], 0.0)

    def pick(when_odd, when_even, slot_odd, slot_even, valid):
        return jnp.where(
            odd == 1, weight(slot_odd, when_odd, valid), weight(slot_even, when_even, valid)
        )

    always = half > 1
    own_w = wts[1, chan]
    near_w = pick(chan, chan, 0, 2, always)
    far_w = pick(chan, chan, 2, 0, has_to)
    from_near_w = pick(near, near, 2, 0, always)
    from_next_w = pick(chan + 1, chan - 1, 0, 2, has_to)
    from_far_w = pick(chan - 2, chan + 2, 2, 0, has_from)
    live_count = live[0, 0]

    def span(first, count):
        if isinstance(first, int):
            return pl.ds(first, count)
        return pl.ds(pl.multiple_of(first, count), count)

    def at(k):
        return span(k * chunk, chunk)

    def alive(first, count, columns):
        ids = lax.broadcasted_iota(jnp.int32, (count, columns), 0) + first
        return ids < live_count

    def masked(first, count):
        return amp[span(first, count)] * alive(first, count, 1).astype(jnp.bfloat16)

    def product(k, slot):
        return jnp.dot(amp[at(k)], hole[slot], preferred_element_type=jnp.float32)

    def remote(src, dst, send, recv, target):
        return pltpu.make_async_remote_copy(
            src_ref=src, dst_ref=dst, send_sem=send, recv_sem=recv,
            device_id=target, device_id_type=MESH,
        )

    def item(k):
        return k + ahead

    def far_copy(i, where):
        return remote(far_out.at[where], far_in.at[where], far_s.at[i], far_r.at[i], {"ja": far_to})

    def near_copy(i, where):
        return remote(near_out.at[where], near_in.at[where], near_s.at[i], near_r.at[i], {"ja": near})

    def side_copy(k):
        return remote(side_out.at[at(k)], side_in.at[at(k)], side_s.at[k], side_r.at[k], {"pt": side})

    def inter_copy(m):
        return remote(inter.at[m], mix_in.at[m], inter_s.at[m], inter_r.at[m], {"pt": side})

    def raw_copy(m):
        return remote(mix_in.at[m], raw_in.at[m], raw_s.at[m], raw_r.at[m], {"ja": near})

    def fwd_copy(m):
        return remote(raw_in.at[m], fwd_in.at[m], fwd_s.at[m], fwd_r.at[m], {"ja": far_from})

    def cfar_copy(m):
        return remote(mix_in.at[raw + m], cfar_in.at[m], cfar_s.at[m], cfar_r.at[m], {"ja": far_to})

    def cnear_copy(m):
        return remote(cnear_out.at[m], cnear_in.at[m], cnear_s.at[m], cnear_r.at[m], {"ja": near})

    def ext_copy():
        return remote(far_out.at[direct], ext_in, ext_s.at[0], ext_r.at[0], {"ja": near})

    def next_copy():
        return remote(ext_in, next_in, next_s.at[0], next_r.at[0], {"ja": far_from})

    def sub_span(i):
        return pl.ds(*subs[i])

    def chunk_copies(make, k):
        if isinstance(k, int) and k in first_items:
            lowest = 1 if make is far_copy else 0
            return [make(i, sub_span(i)) for i in first_items[k] if i >= lowest]
        return [make(item(k), at(k))]

    def send_far(k):
        far_out[at(k)] = (far_w * product(k, far_slot)).astype(jnp.bfloat16)
        for copy in chunk_copies(far_copy, k):
            copy.start()

    def send_near(i, where, there):
        @pl.when(has_from)
        def _():
            far_copy(i, where).wait_recv()

        @pl.when(jnp.logical_not(has_from))
        def _():
            far_in[where] = jnp.zeros((there.size, holes), jnp.bfloat16)

        value = near_p[there] + far_in[where].astype(jnp.float32)
        near_out[where] = value.astype(jnp.bfloat16)
        near_copy(i, where).start()

    def send_side(k):
        side_p[...] = own_w * product(k, 1)
        if isinstance(k, int) and k == 0:
            @pl.when(has_to)
            def _():
                next_copy().wait_recv()
                side_p[direct] = side_p[direct] + next_in[...].astype(jnp.float32)

        for copy in chunk_copies(near_copy, k):
            copy.wait_recv()
        value = side_p[...] + near_in[at(k)].astype(jnp.float32)
        side_out[at(k)] = value.astype(jnp.bfloat16)
        side_copy(k).start()

    def finish(k):
        side_copy(k).wait_recv()
        where = at(k)
        value = jnp.dot(amp[where], mix[...], preferred_element_type=jnp.float32)
        value = value + side_in[where, :wide].astype(jnp.float32)
        value = jnp.where(alive(k * chunk, chunk, 1), value, jnp.zeros_like(value))
        out[where, :wide] = value.astype(jnp.bfloat16)
        out[where, wide:] = side_in[where, wide:]

    head_copy().wait()
    amp[pl.ds(0, 2 * chunk)] = masked(0, 2 * chunk)

    @pl.when(has_to)
    def _():
        hole_copy(far_slot).wait()

    pl.semaphore_wait(barrier, 2 + has_to.astype(jnp.int32) + has_from.astype(jnp.int32))

    @pl.when(has_to)
    def _():
        send_far(0)
        send_far(1)

    hole_copy(near_slot).wait()
    for k in range(2):
        near_p[at(k)] = near_w * product(k, near_slot)

    near_out[direct] = near_p[direct].astype(jnp.bfloat16)
    near_copy(0, direct).start()

    @pl.when(has_to)
    def _():
        ext_copy().start()

    @pl.when(jnp.logical_not(has_from))
    def _():
        for i in range(1, len(subs)):
            where = sub_span(i)
            near_out[where] = near_p[where].astype(jnp.bfloat16)
            near_copy(i, where).start()

    def late_far(k):
        @pl.when(has_to)
        def _():
            send_far(k)

    for b in range(gathers):
        amp_copy(b).wait()
        part_copy(b).wait()
        where = pl.ds(b * gather_rows, gather_rows)
        value = masked(b * gather_rows, gather_rows)
        amp[where] = value
        value = lax.dot_general(
            value, part[where], (((0,), (0,)), ((), ())), preferred_element_type=jnp.float32,
        )
        if b:
            value = acc[...] + value
        if b < gathers - 1:
            acc[...] = value
            continue
        for m in range(mixes):
            inter[m] = value[:, m * width:(m + 1) * width].astype(jnp.bfloat16)
            inter_copy(m).start()

    behind = {1: (2,), 2: (3,), 3: (4,)}
    for i in range(1, len(subs)):
        @pl.when(has_from)
        def _():
            where = sub_span(i)
            far_copy(i, where).wait_recv()
            value = near_p[where] + far_in[where].astype(jnp.float32)
            near_out[where] = value.astype(jnp.bfloat16)
            near_copy(i, where).start()

        for k in behind.get(i, ()):
            late_far(k)
    @pl.when(has_from)
    def _():
        ext_copy().wait_recv()
        next_copy().start()

    hole_copy(1).wait()

    def step(t, far=True, finishing=False):
        if far:
            late_far(t + HEAD)
        near_p[:chunk] = near_w * product(t, near_slot)
        send_near(item(t), at(t), pl.ds(0, chunk))
        send_side(t - GAP)
        if finishing:
            finish(t - LAG)

    for m in range(raw):
        inter_copy(m).wait_recv()
        raw_copy(m).start()
    step(2)
    step(3)
    for m in range(raw):
        raw_copy(m).wait_recv()

        @pl.when(has_from)
        def _():
            fwd_copy(m).start()

    for m in range(raw, mixes):
        inter_copy(m).wait_recv()

    pl.loop(4, LAG)(step)

    for m in range(raw):
        @pl.when(has_to)
        def _():
            fwd_copy(m).wait_recv()

        @pl.when(jnp.logical_not(has_to))
        def _():
            fwd_in[m] = jnp.zeros((holes, width), jnp.bfloat16)

        value = own_w * mix_in[m].astype(jnp.float32)
        value = value + from_near_w * raw_in[m].astype(jnp.float32)
        value = value + from_next_w * fwd_in[m].astype(jnp.float32)
        mix[:, m * width:(m + 1) * width] = value.astype(jnp.bfloat16)

    pl.loop(LAG, terms - HEAD)(functools.partial(step, finishing=True))

    for m in range(tail):
        @pl.when(has_to)
        def _():
            cfar_copy(m).start()

    pl.loop(terms - HEAD, terms)(functools.partial(step, far=False, finishing=True))

    for m in range(tail):
        @pl.when(has_from)
        def _():
            cfar_copy(m).wait_recv()

        @pl.when(jnp.logical_not(has_from))
        def _():
            cfar_in[m] = jnp.zeros((holes, width), jnp.bfloat16)

        value = near_w * mix_in[raw + m].astype(jnp.float32)
        value = value + from_far_w * cfar_in[m].astype(jnp.float32)
        cnear_out[m] = value.astype(jnp.bfloat16)
        cnear_copy(m).start()

    for k in range(terms - GAP, terms):
        send_side(k)

    pl.loop(terms - LAG, terms - 2)(finish)

    finish(terms - 2)

    @pl.when(has_to)
    def _():
        for k in range(2):
            for copy in chunk_copies(far_copy, k):
                copy.wait_send()

        @pl.loop(2, terms)
        def _(k):
            far_copy(item(k), at(k)).wait_send()

        for n in range(tail):
            cfar_copy(n).wait_send()
        ext_copy().wait_send()

    @pl.when(has_from)
    def _():
        for n in range(raw):
            fwd_copy(n).wait_send()
        next_copy().wait_send()

    for n in range(mixes):
        inter_copy(n).wait_send()
    for n in range(raw):
        raw_copy(n).wait_send()
    for k in range(2):
        for copy in chunk_copies(near_copy, k):
            copy.wait_send()

    @pl.loop(2, terms)
    def _(k):
        near_copy(item(k), at(k)).wait_send()

    @pl.loop(0, terms - 2)
    def _(k):
        side_copy(k).wait_send()

    for m in range(tail):
        cnear_copy(m).wait_recv()
        value = own_w * mix_in[raw + m].astype(jnp.float32) + cnear_in[m].astype(jnp.float32)
        late[:, m * width:(m + 1) * width] = value.astype(jnp.bfloat16)

    finish(terms - 1)

    for k in range(terms - 2, terms):
        side_copy(k).wait_send()
    for m in range(tail):
        cnear_copy(m).wait_send()


def closing(steps, live, first, amp, late, out, stage, sems):
    rows = amp.shape[0]
    wide = amp.shape[1] - late.shape[1]
    count = rows // steps
    live_count = live[0, 0]
    copies = []
    for b in range(steps):
        where = pl.ds(b * count, count)
        columns = pl.ds(0, wide)
        copy = pltpu.make_async_copy(
            first.at[where, columns], out.at[0, 0, where, columns], sems.at[steps + b]
        )
        copy.start()
        copies.append(copy)
    for b in range(steps):
        where = pl.ds(b * count, count)
        value = jnp.dot(amp[where], late[...], preferred_element_type=jnp.float32)
        value = value + first[where, wide:].astype(jnp.float32)
        ids = lax.broadcasted_iota(jnp.int32, (count, 1), 0) + b * count
        value = jnp.where(ids < live_count, value, jnp.zeros_like(value))
        stage[where] = value.astype(jnp.bfloat16)
        copy = pltpu.make_async_copy(
            stage.at[where], out.at[0, 0, where, pl.ds(wide, late.shape[1])], sems.at[b]
        )
        copy.start()
        copies.append(copy)
    for copy in copies:
        copy.wait()


def shards(half, amplitudes, live_rows, hole_coupling, part_hole, recoupling):
    rows, holes = amplitudes.shape[2:]
    chunk, block = min(CHUNK, holes), min(BLOCK, rows)
    gather = min(GATHER, rows)
    width = min(128, holes)
    mixes = holes // width
    raw = mixes // 2
    tail = mixes - raw
    terms = rows // chunk
    bf = jnp.bfloat16
    stream = pltpu.VMEM((rows, holes), bf)

    def panels(count):
        return pltpu.VMEM((count, holes, width), bf)

    sems = pltpu.SemaphoreType.DMA
    flops = 10 * rows * holes * holes
    first, amp, late = pl.pallas_call(
        functools.partial(kernel, half, chunk, block, gather, raw),
        out_shape=(
            pltpu.VMEM((rows, holes), bf),
            pltpu.VMEM((rows, holes), bf),
            pltpu.VMEM((holes, tail * width), bf),
        ),
        in_specs=[pl.BlockSpec(memory_space=pltpu.SMEM)] * 2
        + [pl.BlockSpec(memory_space=pl.ANY)] * 3,
        out_specs=[pl.BlockSpec(memory_space=pltpu.VMEM)] * 3,
        scratch_shapes=[
            pltpu.VMEM((3, holes, holes), bf),
            pltpu.VMEM((rows, holes), bf),
            pltpu.VMEM((holes, holes), jnp.float32),
            panels(mixes), panels(mixes), panels(raw), panels(raw),
            panels(tail), panels(tail), panels(tail),
            pltpu.VMEM((holes, raw * width), bf),
            pltpu.VMEM((chunk // 2, holes), bf),
            pltpu.VMEM((chunk // 2, holes), bf),
            stream, stream, stream, stream, stream, stream,
            pltpu.VMEM((2 * chunk, holes), jnp.float32),
            pltpu.VMEM((chunk, holes), jnp.float32),
            sems((rows // gather + 1,)),
            sems((rows // gather,)),
            sems((3,)),
            sems((terms + 3,)), sems((terms + 3,)), sems((terms + 3,)), sems((terms + 3,)),
            sems((terms,)), sems((terms,)),
            sems((mixes,)), sems((mixes,)),
            sems((raw,)), sems((raw,)), sems((raw,)), sems((raw,)),
            sems((tail,)), sems((tail,)), sems((tail,)), sems((tail,)),
            sems((1,)), sems((1,)), sems((1,)), sems((1,)),
        ],
        compiler_params=pltpu.CompilerParams(
            collective_id=0, has_side_effects=True, vmem_limit_bytes=56 << 20
        ),
        cost_estimate=pl.CostEstimate(
            flops=flops, bytes_accessed=6 * rows * holes * 2, transcendentals=0
        ),
        name="gt_bar",
    )(recoupling.T, live_rows, amplitudes, hole_coupling, part_hole)
    return pl.pallas_call(
        functools.partial(closing, STEPS),
        out_shape=jax.ShapeDtypeStruct(amplitudes.shape, bf),
        in_specs=[pl.BlockSpec(memory_space=pltpu.SMEM)]
        + [pl.BlockSpec(memory_space=pltpu.VMEM)] * 3,
        out_specs=pl.BlockSpec(memory_space=pl.ANY),
        scratch_shapes=[pltpu.VMEM((rows, tail * width), bf), sems((2 * STEPS,))],
        compiler_params=pltpu.CompilerParams(vmem_limit_bytes=24 << 20),
        cost_estimate=pl.CostEstimate(
            flops=flops // 10, bytes_accessed=2 * rows * holes * 2, transcendentals=0
        ),
        name="gt_close",
    )(live_rows, first, amp, late)


def solution(mesh):
    in_specs = (
        P("ja", "pt", None, None),
        P("ja", "pt"),
        P("ja", "pt", None, None, None),
        P("ja", "pt", None, None),
        P(),
    )
    out_specs = P("ja", "pt", None, None)
    body = functools.partial(shards, mesh.shape["ja"] // 2)
    return jax.shard_map(body, mesh=mesh, in_specs=in_specs, out_specs=out_specs, check_vma=False)
```

```python
import functools

import jax
import jax.numpy as jnp
from jax import lax
from jax.experimental import pallas as pl
from jax.experimental.pallas import tpu as pltpu
from jax.sharding import PartitionSpec as P

MESH = pl.DeviceIdType.MESH
CHUNK = 128
BLOCK = 512
GATHER = (5, 4, 3)
HEAD = 3
GAP = 2
LAG = 9
STEPS = 3


def kernel(
    half, chunk, block, gather_rows, raw,
    wts, live, amp_hbm, hole_hbm, part_hbm, out, amp, late,
    hole, part, acc, inter, mix_in, raw_in, fwd_in, cfar_in, cnear_out, cnear_in, mix,
    ext_in, next_in,
    far_out, far_in, near_out, near_in, side_out, side_in, near_p, side_p,
    amp_sem, part_sem, hole_sem,
    far_s, far_r, near_s, near_r, side_s, side_r, inter_s, inter_r,
    raw_s, raw_r, fwd_s, fwd_r, cfar_s, cfar_r, cnear_s, cnear_r,
    ext_s, ext_r, next_s, next_r,
):
    rows, holes = amp.shape
    terms = rows // chunk
    blocks = rows // block
    gathers = len(gather_rows)
    starts = [sum(gather_rows[:b]) for b in range(gathers)]
    mixes, _, width = inter.shape
    tail = mixes - raw
    wide = raw * width
    quarter, mid = chunk // 4, chunk // 2
    subs = [
        (0, mid), (mid, quarter), (mid + quarter, quarter), (chunk, mid), (chunk + mid, mid)
    ]
    first_items = {0: range(0, 3), 1: range(3, 5)}
    ahead = len(subs) - 2
    direct = pl.ds(0, mid)

    chans = wts.shape[1]
    chan = lax.axis_index("ja")
    label = lax.axis_index("pt")
    pos = lax.rem(chan, half)
    base = chan - pos
    odd = lax.rem(chan, 2)
    sign = 2 * odd - 1
    near = chan - sign
    has_to = jnp.logical_and(pos + 2 * sign >= 0, pos + 2 * sign < half)
    has_from = jnp.logical_and(pos - 2 * sign >= 0, pos - 2 * sign < half)
    far_to = base + lax.rem(pos + half + 2 * sign, half)
    far_from = base + lax.rem(pos + half - 2 * sign, half)
    side = label + 2 - 4 * lax.rem(lax.div(label, 2), 2)

    near_slot = 2 - 2 * odd
    far_slot = 2 * odd

    def amp_copy(b):
        start, size = starts[b], gather_rows[b]
        if b == 0:
            start, size = 2 * chunk, size - 2 * chunk
        part_rows = pl.ds(start, size)
        return pltpu.make_async_copy(amp_hbm.at[0, 0, part_rows], amp.at[part_rows], amp_sem.at[b])

    def head_copy():
        part_rows = pl.ds(0, 2 * chunk)
        return pltpu.make_async_copy(
            amp_hbm.at[0, 0, part_rows], amp.at[part_rows], amp_sem.at[gathers]
        )

    def part_copy(b):
        part_rows = pl.ds(starts[b], gather_rows[b])
        return pltpu.make_async_copy(part_hbm.at[0, 0, part_rows], part.at[part_rows], part_sem.at[b])

    def hole_copy(slot):
        return pltpu.make_async_copy(hole_hbm.at[0, 0, slot], hole.at[slot], hole_sem.at[slot])

    head_copy().start()

    @pl.when(has_to)
    def _():
        hole_copy(far_slot).start()

    hole_copy(near_slot).start()
    for b in range(gathers):
        amp_copy(b).start()
        part_copy(b).start()
    hole_copy(1).start()

    barrier = pltpu.get_barrier_semaphore()
    pl.semaphore_signal(barrier, inc=1, device_id={"ja": near}, device_id_type=MESH)
    pl.semaphore_signal(barrier, inc=1, device_id={"pt": side}, device_id_type=MESH)

    @pl.when(has_to)
    def _():
        pl.semaphore_signal(barrier, inc=1, device_id={"ja": far_to}, device_id_type=MESH)

    @pl.when(has_from)
    def _():
        pl.semaphore_signal(barrier, inc=1, device_id={"ja": far_from}, device_id_type=MESH)

    def weight(slot, source, valid):
        clipped = jnp.clip(source, 0, chans - 1)
        return jnp.where(valid, wts[slot, clipped], 0.0)

    def pick(when_odd, when_even, slot_odd, slot_even, valid):
        return jnp.where(
            odd == 1, weight(slot_odd, when_odd, valid), weight(slot_even, when_even, valid)
        )

    always = half > 1
    own_w = wts[1, chan]
    near_w = pick(chan, chan, 0, 2, always)
    far_w = pick(chan, chan, 2, 0, has_to)
    from_near_w = pick(near, near, 2, 0, always)
    from_next_w = pick(chan + 1, chan - 1, 0, 2, has_to)
    from_far_w = pick(chan - 2, chan + 2, 2, 0, has_from)
    live_count = live[0, 0]

    def span(first, count):
        if isinstance(first, int):
            return pl.ds(first, count)
        return pl.ds(pl.multiple_of(first, count), count)

    def at(k):
        return span(k * chunk, chunk)

    def alive(first, count, columns):
        ids = lax.broadcasted_iota(jnp.int32, (count, columns), 0) + first
        return ids < live_count

    def masked(first, count):
        return amp[span(first, count)] * alive(first, count, 1).astype(jnp.bfloat16)

    def product(k, slot):
        return jnp.dot(amp[at(k)], hole[slot], preferred_element_type=jnp.float32)

    def remote(src, dst, send, recv, target):
        return pltpu.make_async_remote_copy(
            src_ref=src, dst_ref=dst, send_sem=send, recv_sem=recv,
            device_id=target, device_id_type=MESH,
        )

    def item(k):
        return k + ahead

    def far_copy(i, where):
        return remote(far_out.at[where], far_in.at[where], far_s.at[i], far_r.at[i], {"ja": far_to})

    def near_copy(i, where):
        return remote(near_out.at[where], near_in.at[where], near_s.at[i], near_r.at[i], {"ja": near})

    def side_copy(k):
        return remote(side_out.at[at(k)], side_in.at[at(k)], side_s.at[k], side_r.at[k], {"pt": side})

    def inter_copy(m):
        return remote(inter.at[m], mix_in.at[m], inter_s.at[m], inter_r.at[m], {"pt": side})

    def raw_copy(m):
        return remote(mix_in.at[m], raw_in.at[m], raw_s.at[m], raw_r.at[m], {"ja": near})

    def fwd_copy(m):
        return remote(raw_in.at[m], fwd_in.at[m], fwd_s.at[m], fwd_r.at[m], {"ja": far_from})

    def cfar_copy(m):
        return remote(mix_in.at[raw + m], cfar_in.at[m], cfar_s.at[m], cfar_r.at[m], {"ja": far_to})

    def cnear_copy(m):
        return remote(cnear_out.at[m], cnear_in.at[m], cnear_s.at[m], cnear_r.at[m], {"ja": near})

    def ext_copy():
        return remote(far_out.at[direct], ext_in, ext_s.at[0], ext_r.at[0], {"ja": near})

    def next_copy():
        return remote(ext_in, next_in, next_s.at[0], next_r.at[0], {"ja": far_from})

    def sub_span(i):
        return pl.ds(*subs[i])

    def chunk_copies(make, k):
        if isinstance(k, int) and k in first_items:
            lowest = 1 if make is far_copy else 0
            return [make(i, sub_span(i)) for i in first_items[k] if i >= lowest]
        return [make(item(k), at(k))]

    def send_far(k):
        far_out[at(k)] = (far_w * product(k, far_slot)).astype(jnp.bfloat16)
        for copy in chunk_copies(far_copy, k):
            copy.start()

    def send_near(i, where, there):
        @pl.when(has_from)
        def _():
            far_copy(i, where).wait_recv()

        @pl.when(jnp.logical_not(has_from))
        def _():
            far_in[where] = jnp.zeros((there.size, holes), jnp.bfloat16)

        value = near_p[there] + far_in[where].astype(jnp.float32)
        near_out[where] = value.astype(jnp.bfloat16)
        near_copy(i, where).start()

    def send_side(k):
        side_p[...] = own_w * product(k, 1)
        if isinstance(k, int) and k == 0:
            @pl.when(has_to)
            def _():
                next_copy().wait_recv()
                side_p[direct] = side_p[direct] + next_in[...].astype(jnp.float32)

        for copy in chunk_copies(near_copy, k):
            copy.wait_recv()
        value = side_p[...] + near_in[at(k)].astype(jnp.float32)
        side_out[at(k)] = value.astype(jnp.bfloat16)
        side_copy(k).start()

    def finish(k):
        side_copy(k).wait_recv()
        where = at(k)
        value = jnp.dot(amp[where], mix[...], preferred_element_type=jnp.float32)
        value = value + side_in[where, :wide].astype(jnp.float32)
        value = jnp.where(alive(k * chunk, chunk, 1), value, jnp.zeros_like(value))
        out[where, :wide] = value.astype(jnp.bfloat16)
        out[where, wide:] = side_in[where, wide:]

    head_copy().wait()
    amp[pl.ds(0, 2 * chunk)] = masked(0, 2 * chunk)

    @pl.when(has_to)
    def _():
        hole_copy(far_slot).wait()

    pl.semaphore_wait(barrier, 2 + has_to.astype(jnp.int32) + has_from.astype(jnp.int32))

    @pl.when(has_to)
    def _():
        send_far(0)
        send_far(1)

    hole_copy(near_slot).wait()
    for k in range(2):
        near_p[at(k)] = near_w * product(k, near_slot)

    near_out[direct] = near_p[direct].astype(jnp.bfloat16)
    near_copy(0, direct).start()

    @pl.when(has_to)
    def _():
        ext_copy().start()

    @pl.when(jnp.logical_not(has_from))
    def _():
        for i in range(1, len(subs)):
            where = sub_span(i)
            near_out[where] = near_p[where].astype(jnp.bfloat16)
            near_copy(i, where).start()

    def late_far(k):
        @pl.when(has_to)
        def _():
            send_far(k)

    for b in range(gathers):
        amp_copy(b).wait()
        part_copy(b).wait()
        where = pl.ds(starts[b], gather_rows[b])
        value = masked(starts[b], gather_rows[b])
        amp[where] = value
        def gathered(columns):
            return lax.dot_general(
                value, part[where, columns],
                (((0,), (0,)), ((), ())), preferred_element_type=jnp.float32,
            )

        if b < gathers - 1:
            term = gathered(slice(0, holes))
            acc[...] = acc[...] + term if b else term
            continue
        for low, high in ((0, raw), (raw, mixes)):
            columns = slice(low * width, high * width)
            term = gathered(columns)
            if b:
                term = acc[:, columns] + term
            for m in range(low, high):
                first = (m - low) * width
                inter[m] = term[:, first:first + width].astype(jnp.bfloat16)
                inter_copy(m).start()

    behind = {1: (2,), 2: (3,), 3: (4,)}
    for i in range(1, len(subs)):
        @pl.when(has_from)
        def _():
            where = sub_span(i)
            far_copy(i, where).wait_recv()
            value = near_p[where] + far_in[where].astype(jnp.float32)
            near_out[where] = value.astype(jnp.bfloat16)
            near_copy(i, where).start()

        for k in behind.get(i, ()):
            late_far(k)
    @pl.when(has_from)
    def _():
        ext_copy().wait_recv()
        next_copy().start()

    hole_copy(1).wait()

    def step(t, far=True, finishing=False):
        if far:
            late_far(t + HEAD)
        near_p[:chunk] = near_w * product(t, near_slot)
        send_near(item(t), at(t), pl.ds(0, chunk))
        send_side(t - GAP)
        if finishing:
            finish(t - LAG)

    for m in range(raw):
        inter_copy(m).wait_recv()
        raw_copy(m).start()
    step(2)
    step(3)
    for m in range(raw):
        raw_copy(m).wait_recv()

        @pl.when(has_from)
        def _():
            fwd_copy(m).start()

    for m in range(raw, mixes):
        inter_copy(m).wait_recv()

    pl.loop(4, LAG)(step)

    for m in range(raw):
        @pl.when(has_to)
        def _():
            fwd_copy(m).wait_recv()

        @pl.when(jnp.logical_not(has_to))
        def _():
            fwd_in[m] = jnp.zeros((holes, width), jnp.bfloat16)

        value = own_w * mix_in[m].astype(jnp.float32)
        value = value + from_near_w * raw_in[m].astype(jnp.float32)
        value = value + from_next_w * fwd_in[m].astype(jnp.float32)
        mix[:, m * width:(m + 1) * width] = value.astype(jnp.bfloat16)

    pl.loop(LAG, terms - HEAD)(functools.partial(step, finishing=True))

    for m in range(tail):
        @pl.when(has_to)
        def _():
            cfar_copy(m).start()

    pl.loop(terms - HEAD, terms)(functools.partial(step, far=False, finishing=True))

    for m in range(tail):
        @pl.when(has_from)
        def _():
            cfar_copy(m).wait_recv()

        @pl.when(jnp.logical_not(has_from))
        def _():
            cfar_in[m] = jnp.zeros((holes, width), jnp.bfloat16)

        value = near_w * mix_in[raw + m].astype(jnp.float32)
        value = value + from_far_w * cfar_in[m].astype(jnp.float32)
        cnear_out[m] = value.astype(jnp.bfloat16)
        cnear_copy(m).start()

    for k in range(terms - GAP, terms):
        send_side(k)

    pl.loop(terms - LAG, terms - 2)(finish)

    finish(terms - 2)

    @pl.when(has_to)
    def _():
        for k in range(2):
            for copy in chunk_copies(far_copy, k):
                copy.wait_send()

        @pl.loop(2, terms)
        def _(k):
            far_copy(item(k), at(k)).wait_send()

        for n in range(tail):
            cfar_copy(n).wait_send()
        ext_copy().wait_send()

    @pl.when(has_from)
    def _():
        for n in range(raw):
            fwd_copy(n).wait_send()
        next_copy().wait_send()

    for n in range(mixes):
        inter_copy(n).wait_send()
    for n in range(raw):
        raw_copy(n).wait_send()
    for k in range(2):
        for copy in chunk_copies(near_copy, k):
            copy.wait_send()

    @pl.loop(2, terms)
    def _(k):
        near_copy(item(k), at(k)).wait_send()

    @pl.loop(0, terms - 2)
    def _(k):
        side_copy(k).wait_send()

    for m in range(tail):
        cnear_copy(m).wait_recv()
        value = own_w * mix_in[raw + m].astype(jnp.float32) + cnear_in[m].astype(jnp.float32)
        late[:, m * width:(m + 1) * width] = value.astype(jnp.bfloat16)

    finish(terms - 1)

    for k in range(terms - 2, terms):
        side_copy(k).wait_send()
    for m in range(tail):
        cnear_copy(m).wait_send()


def closing(steps, live, first, amp, late, out, stage, sems):
    rows = amp.shape[0]
    wide = amp.shape[1] - late.shape[1]
    count = rows // steps
    live_count = live[0, 0]
    copies = []
    for b in range(steps):
        where = pl.ds(b * count, count)
        columns = pl.ds(0, wide)
        copy = pltpu.make_async_copy(
            first.at[where, columns], out.at[0, 0, where, columns], sems.at[steps + b]
        )
        copy.start()
        copies.append(copy)
    for b in range(steps):
        where = pl.ds(b * count, count)
        value = jnp.dot(amp[where], late[...], preferred_element_type=jnp.float32)
        value = value + first[where, wide:].astype(jnp.float32)
        ids = lax.broadcasted_iota(jnp.int32, (count, 1), 0) + b * count
        value = jnp.where(ids < live_count, value, jnp.zeros_like(value))
        stage[where] = value.astype(jnp.bfloat16)
        copy = pltpu.make_async_copy(
            stage.at[where], out.at[0, 0, where, pl.ds(wide, late.shape[1])], sems.at[b]
        )
        copy.start()
        copies.append(copy)
    for copy in copies:
        copy.wait()


def shards(half, amplitudes, live_rows, hole_coupling, part_hole, recoupling):
    rows, holes = amplitudes.shape[2:]
    chunk, block = min(CHUNK, holes), min(BLOCK, rows)
    gather = [rows * part // 12 for part in GATHER]
    width = min(128, holes)
    mixes = holes // width
    raw = mixes // 2
    tail = mixes - raw
    terms = rows // chunk
    bf = jnp.bfloat16
    stream = pltpu.VMEM((rows, holes), bf)

    def panels(count):
        return pltpu.VMEM((count, holes, width), bf)

    sems = pltpu.SemaphoreType.DMA
    flops = 10 * rows * holes * holes
    first, amp, late = pl.pallas_call(
        functools.partial(kernel, half, chunk, block, gather, raw),
        out_shape=(
            pltpu.VMEM((rows, holes), bf),
            pltpu.VMEM((rows, holes), bf),
            pltpu.VMEM((holes, tail * width), bf),
        ),
        in_specs=[pl.BlockSpec(memory_space=pltpu.SMEM)] * 2
        + [pl.BlockSpec(memory_space=pl.ANY)] * 3,
        out_specs=[pl.BlockSpec(memory_space=pltpu.VMEM)] * 3,
        scratch_shapes=[
            pltpu.VMEM((3, holes, holes), bf),
            pltpu.VMEM((rows, holes), bf),
            pltpu.VMEM((holes, holes), jnp.float32),
            panels(mixes), panels(mixes), panels(raw), panels(raw),
            panels(tail), panels(tail), panels(tail),
            pltpu.VMEM((holes, raw * width), bf),
            pltpu.VMEM((chunk // 2, holes), bf),
            pltpu.VMEM((chunk // 2, holes), bf),
            stream, stream, stream, stream, stream, stream,
            pltpu.VMEM((2 * chunk, holes), jnp.float32),
            pltpu.VMEM((chunk, holes), jnp.float32),
            sems((len(gather) + 1,)),
            sems((len(gather),)),
            sems((3,)),
            sems((terms + 3,)), sems((terms + 3,)), sems((terms + 3,)), sems((terms + 3,)),
            sems((terms,)), sems((terms,)),
            sems((mixes,)), sems((mixes,)),
            sems((raw,)), sems((raw,)), sems((raw,)), sems((raw,)),
            sems((tail,)), sems((tail,)), sems((tail,)), sems((tail,)),
            sems((1,)), sems((1,)), sems((1,)), sems((1,)),
        ],
        compiler_params=pltpu.CompilerParams(
            collective_id=0, has_side_effects=True, vmem_limit_bytes=56 << 20
        ),
        cost_estimate=pl.CostEstimate(
            flops=flops, bytes_accessed=6 * rows * holes * 2, transcendentals=0
        ),
        name="gt_bar",
    )(recoupling.T, live_rows, amplitudes, hole_coupling, part_hole)
    return pl.pallas_call(
        functools.partial(closing, STEPS),
        out_shape=jax.ShapeDtypeStruct(amplitudes.shape, bf),
        in_specs=[pl.BlockSpec(memory_space=pltpu.SMEM)]
        + [pl.BlockSpec(memory_space=pltpu.VMEM)] * 3,
        out_specs=pl.BlockSpec(memory_space=pl.ANY),
        scratch_shapes=[pltpu.VMEM((rows, tail * width), bf), sems((2 * STEPS,))],
        compiler_params=pltpu.CompilerParams(vmem_limit_bytes=24 << 20),
        cost_estimate=pl.CostEstimate(
            flops=flops // 10, bytes_accessed=2 * rows * holes * 2, transcendentals=0
        ),
        name="gt_close",
    )(live_rows, first, amp, late)


def solution(mesh):
    in_specs = (
        P("ja", "pt", None, None),
        P("ja", "pt"),
        P("ja", "pt", None, None, None),
        P("ja", "pt", None, None),
        P(),
    )
    out_specs = P("ja", "pt", None, None)
    body = functools.partial(shards, mesh.shape["ja"] // 2)
    return jax.shard_map(body, mesh=mesh, in_specs=in_specs, out_specs=out_specs, check_vma=False)
```
